32 devices in a mesh: lon: 8 (over y, x, core), lev: 4 (over z).
Axes of the slice: x: 2, y: 2, z: 4, core: 2. Of those that a mesh axis runs over, the one named last changes fastest.
Arguments:
- tracers: float32 [32, 16, 64, 1024], P(None, 'lev', None, 'lon'), may hold values from 0.1 to 10
- offsets: int32 [64], replicated, may hold values from 0 to 1023
- fraction: float32 [64], replicated, may hold values from 0 to 1
- bin_class: int32 [8], replicated, may hold values from 0 to 7
- thickness: float32 [16], P('lev'), may hold values from 0.5 to 2
Outputs:
- settled: float32 [32, 16, 64, 1024], P(None, 'lev', None, 'lon')
The draws below stay inside these ranges and needn't reach their ends.
All inputs are finite; a program needn't handle non-finite values.
Results may differ from the reference program's by a relative error of at most 0.00002.
Values sent between devices are 32-bit elements; how exact they have to be, the bound alone decides.
A program may use at most 128 MiB of HBM per device.

```python
import math
import jax
import jax.numpy as jnp
from jax import lax

GROUPS = 4
TRACERS = 32
NCLASS = 8
NLAT = 64
WBINS = 8
NLON = 1024
NLEV = 16


def touch_ends(array, key, smallest, high):
    index_at = [jax.random.randint(jax.random.fold_in(key, axis), (), 0, length) for axis, length in enumerate(array.shape)]
    longest = array.shape.index(max(array.shape))
    next_to = index_at[:longest] + [(index_at[longest] + 1) % array.shape[longest]] + index_at[longest + 1:]
    return array.at[tuple(index_at)].set(smallest).at[tuple(next_to)].set(high)


def block_scale(stream_key, dims, shards, low, largest):
    gain, own = 1.0, jax.random.fold_in(stream_key, 6)
    for position, shards_of in shards:
        heights = jnp.exp(jax.random.uniform(jax.random.fold_in(own, position), (shards_of,), jnp.float32, low / len(shards), largest / len(shards)))
        gain = gain * jnp.repeat(heights, dims[position] // shards_of).reshape([-1 if axis == position else 1 for axis in range(len(dims))])
    return gain


def setup_inputs(seed: int = 0) -> dict:
    splits = jax.random.split(jax.random.key(seed), 6)
    return {
        "tracers": jnp.clip(jnp.exp(math.log(10.0) - 4.6051702 * jax.random.uniform(splits[0], (TRACERS, NLEV, NLAT, NLON), jnp.float32) ** block_scale(splits[0], (TRACERS, NLEV, NLAT, NLON), ((1, 4), (3, 8)), -0.2, 0.2)), 0.1, 10.0),
        "offsets": touch_ends(jax.random.randint(splits[1], (NLAT,), 0, NLON), jax.random.fold_in(splits[1], 1), 0, NLON - 1).astype(jnp.int32),
        "fraction": jnp.clip(jax.random.uniform(splits[2], (NLAT,), jnp.float32, 0.0, 1.0), 0.0, 1.0),
        "bin_class": touch_ends(jax.random.randint(splits[3], (WBINS,), 0, NCLASS), jax.random.fold_in(splits[3], 1), 0, NCLASS - 1).astype(jnp.int32),
        "thickness": jnp.clip(jnp.exp(math.log(2.0) - 1.3862944 * jax.random.uniform(splits[4], (NLEV,), jnp.float32) ** block_scale(splits[4], (NLEV,), ((0, 4),), -0.2, 0.2)), 0.5, 2.0),
    }


def reference(tracers, offsets, fraction, bin_class, thickness):
    nlon = tracers.shape[-1]
    nlat = tracers.shape[2]
    cells = jnp.arange(nlon, dtype=jnp.int32)
    first = (cells[None, :] - offsets[:, None]) % nlon
    second = (first - 1) % nlon
    rows = jnp.arange(nlat, dtype=jnp.int32)[:, None]
    share = fraction[:, None]

    def move(field):
        return (1.0 - share) * field[:, rows, first] + share * field[:, rows, second]

    moved = lax.map(move, tracers)
    speed = 0.5 * jnp.exp2(jnp.repeat(bin_class, GROUPS).astype(jnp.float32))
    ratio = speed[:, None] / thickness[None, :]

    def level(carry, inputs):
        column, rate = inputs
        rate = rate[:, None, None]
        value = (column + rate * carry) / (1.0 + rate)
        return value, value

    start = jnp.zeros((tracers.shape[0], nlat, nlon), jnp.float32)
    _, settled = lax.scan(level, start, (jnp.swapaxes(moved, 0, 1), ratio.T))
    return jnp.swapaxes(settled, 0, 1)
```

```python
import functools

import jax
import jax.numpy as jnp
from jax import lax
from jax.experimental import pallas as pl
from jax.experimental.pallas import tpu as pltpu
from jax.sharding import PartitionSpec as P

GROUPS = 4
SUB = 8
PIECES = 8


def exchange_kernel(
    n, depth, x_ref, coef_ref, row_ref, share_ref, out_ref,
    recv, obuf, zin, s1, r1, s2, r2, own1, own2, zs, zr,
):
    tracers, levels, lats, width = x_ref.shape
    mine = tracers // n
    halves = max(1, min(PIECES // mine, lats // SUB))
    rows_of = lats // halves
    me = lax.axis_index("lon")
    lev = lax.axis_index("lev")

    def at(c):
        return c // halves, pl.ds(pl.multiple_of((c % halves) * rows_of, SUB), rows_of)

    def peer(k):
        return lax.rem(me + k, n)

    def outward(c, k):
        tt, rows = at(c)
        return pltpu.make_async_remote_copy(
            src_ref=x_ref.at[peer(k) * mine + tt, :, rows, :],
            dst_ref=recv.at[me, tt, :, rows, :],
            send_sem=s1.at[c, k], recv_sem=r1.at[c, k],
            device_id={"lon": peer(k)}, device_id_type=pl.DeviceIdType.MESH,
        )

    def homeward(c, k):
        tt, rows = at(c)
        return pltpu.make_async_remote_copy(
            src_ref=obuf.at[peer(k), tt, :, rows, :],
            dst_ref=out_ref.at[me * mine + tt, :, rows, :],
            send_sem=s2.at[c, k], recv_sem=r2.at[c, k],
            device_id={"lon": peer(k)}, device_id_type=pl.DeviceIdType.MESH,
        )

    def downward(c):
        tt, rows = at(c)
        return pltpu.make_async_remote_copy(
            src_ref=obuf.at[:, tt, levels - 1, rows, :],
            dst_ref=zin.at[:, tt, rows, :],
            send_sem=zs.at[c], recv_sem=zr.at[c],
            device_id={"lev": lax.rem(lev + 1, depth)}, device_id_type=pl.DeviceIdType.MESH,
        )

    def own_in(c):
        tt, rows = at(c)
        return pltpu.make_async_copy(
            x_ref.at[me * mine + tt, :, rows, :], recv.at[me, tt, :, rows, :], own1.at[c])

    def own_out(c):
        tt, rows = at(c)
        return pltpu.make_async_copy(
            obuf.at[me, tt, :, rows, :], out_ref.at[me * mine + tt, :, rows, :], own2.at[c])

    barrier = pltpu.get_barrier_semaphore()
    for k in range(1, n):
        pl.semaphore_signal(barrier, inc=1, device_id={"lon": peer(k)},
                            device_id_type=pl.DeviceIdType.MESH)
    for k in (1, depth - 1):
        pl.semaphore_signal(barrier, inc=1, device_id={"lev": lax.rem(lev + k, depth)},
                            device_id_type=pl.DeviceIdType.MESH)
    pl.semaphore_wait(barrier, n + 1)

    count = mine * halves

    @pl.loop(0, count)
    def _(c):
        own_in(c).start()

        @pl.loop(1, n)
        def _(k):
            outward(c, k).start()

    lane = lax.broadcasted_iota(jnp.int32, (SUB, width), 1)

    def behind(value, by):
        by %= n
        if by == 0:
            return value
        return jnp.concatenate([value[n - by:], value[:n - by]], axis=0)

    @pl.loop(0, count)
    def _(c):
        tt = c // halves
        base = (c % halves) * rows_of
        tracer = me * mine + tt
        own_in(c).wait()

        @pl.loop(1, n)
        def _(k):
            outward(c, k).wait_recv()

        @pl.loop(0, rows_of // SUB)
        def _(g):
            rows = pl.ds(pl.multiple_of(base + g * SUB, SUB), SUB)
            remainder = row_ref[0, rows, :]
            quotient = row_ref[1, rows, :]
            share = share_ref[rows, :]
            fine = [(remainder & (1 << b)) != 0 for b in range((width - 1).bit_length())]
            coarse = [(quotient & (1 << b)) != 0 for b in range((n - 1).bit_length())]
            same_block = lane >= remainder
            first_lane = lane == 0
            value = None
            for level in range(levels):
                field = recv[:, tt, level, rows, :]
                turned = pltpu.roll(field, 1, axis=2)
                left = jnp.where(first_lane[None], behind(turned, 1), turned)
                field = (1.0 - share)[None] * field + share[None] * left
                for b, chosen in enumerate(fine):
                    field = jnp.where(chosen[None], pltpu.roll(field, 1 << b, axis=2), field)
                field = jnp.where(same_block[None], field, behind(field, 1))
                for b, chosen in enumerate(coarse):
                    field = jnp.where(chosen[None], behind(field, 1 << b), field)
                field = coef_ref[0, tracer * levels + level] * field
                value = field if value is None else field + coef_ref[1, tracer * levels + level] * value
                obuf[:, tt, level, rows, :] = value

        def add_above(level):
            @pl.loop(0, rows_of // SUB)
            def _(g):
                rows = pl.ds(pl.multiple_of(base + g * SUB, SUB), SUB)
                obuf[:, tt, level, rows, :] += (
                    coef_ref[2, tracer * levels + level] * zin[:, tt, rows, :])

        @pl.when(lev > 0)
        def _():
            downward(c).wait_recv()
            add_above(levels - 1)

        @pl.when(lev < depth - 1)
        def _():
            downward(c).start()

        @pl.when(lev > 0)
        def _():
            for level in range(levels - 1):
                add_above(level)

        own_out(c).start()

        @pl.loop(1, n)
        def _(k):
            homeward(c, k).start()

    @pl.loop(0, count)
    def _(c):
        own_out(c).wait()

        @pl.when(lev < depth - 1)
        def _():
            downward(c).wait_send()

        @pl.loop(1, n)
        def _(k):
            outward(c, k).wait_send()
            homeward(c, k).wait()


def on_device(tracers, offsets, fraction, bin_class, thickness):
    count, levels, lats, width = tracers.shape
    n = lax.axis_size("lon")
    depth = lax.axis_size("lev")
    mine = count // n
    pieces = mine * max(1, min(PIECES // mine, lats // SUB))
    speed = 0.5 * jnp.exp2(jnp.repeat(bin_class, GROUPS).astype(jnp.float32))
    ratio = speed[:, None] / thickness[None, :]
    keep = 1.0 / (1.0 + ratio)
    carry = ratio * keep
    reach = [carry[:, 0]]
    for level in range(1, levels):
        reach.append(reach[-1] * carry[:, level])
    coef = jnp.stack([keep, carry, jnp.stack(reach, axis=1)]).reshape(3, count * levels)
    row = jnp.broadcast_to(
        jnp.stack([offsets % width, offsets // width])[:, :, None], (2, lats, width))
    share = jnp.broadcast_to(fraction[:, None], (lats, width))
    hbm = pl.BlockSpec(memory_space=pl.ANY)
    vmem = pl.BlockSpec(memory_space=pltpu.VMEM)
    sem = pltpu.SemaphoreType.DMA
    return pl.pallas_call(
        functools.partial(exchange_kernel, n, depth),
        out_shape=jax.ShapeDtypeStruct(tracers.shape, jnp.float32),
        in_specs=[hbm, pl.BlockSpec(memory_space=pltpu.SMEM), vmem, vmem],
        out_specs=hbm,
        scratch_shapes=[
            pltpu.VMEM((n, mine, levels, lats, width), jnp.float32),
            pltpu.VMEM((n, mine, levels, lats, width), jnp.float32),
            pltpu.VMEM((n, mine, lats, width), jnp.float32),
            sem((pieces, n)), sem((pieces, n)), sem((pieces, n)), sem((pieces, n)),
            sem((pieces,)), sem((pieces,)), sem((pieces,)), sem((pieces,)),
        ],
        compiler_params=pltpu.CompilerParams(
            collective_id=0, has_side_effects=True, vmem_limit_bytes=24 << 20),
    )(tracers, coef, row, share)


def solution(mesh):
    in_specs = (P(None, "lev", None, "lon"), P(), P(), P(), P("lev"))
    out_specs = P(None, "lev", None, "lon")
    return jax.shard_map(
        on_device, mesh=mesh, in_specs=in_specs, out_specs=out_specs, check_vma=False
    )
```

```python
import functools

import jax
import jax.numpy as jnp
from jax import lax
from jax.experimental import pallas as pl
from jax.experimental.pallas import tpu as pltpu
from jax.sharding import PartitionSpec as P

GROUPS = 4
SUB = 8
PIECES = 8
HOLD = 5


def exchange_kernel(
    n, depth, x_ref, offsets_ref, fraction_ref, class_ref, thick_ref, out_ref,
    recv, obuf, zin, row_ref, share_ref, s1, r1, s2, r2, own1, own2, zs, zr,
):
    tracers, levels, lats, width = x_ref.shape
    mine = tracers // n
    halves = max(1, min(PIECES // mine, lats // SUB))
    rows_of = lats // halves
    me = lax.axis_index("lon")
    lev = lax.axis_index("lev")

    def at(c):
        return c // halves, pl.ds(pl.multiple_of((c % halves) * rows_of, SUB), rows_of)

    def peer(k):
        return lax.rem(me + k, n)

    def outward(c, k):
        tt, rows = at(c)
        return pltpu.make_async_remote_copy(
            src_ref=x_ref.at[peer(k) * mine + tt, :, rows, :],
            dst_ref=recv.at[me, tt, :, rows, :],
            send_sem=s1.at[c, k], recv_sem=r1.at[c, k],
            device_id={"lon": peer(k)}, device_id_type=pl.DeviceIdType.MESH,
        )

    def homeward(c, k):
        tt, rows = at(c)
        return pltpu.make_async_remote_copy(
            src_ref=obuf.at[peer(k), tt, :, rows, :],
            dst_ref=out_ref.at[me * mine + tt, :, rows, :],
            send_sem=s2.at[c, k], recv_sem=r2.at[c, k],
            device_id={"lon": peer(k)}, device_id_type=pl.DeviceIdType.MESH,
        )

    def downward(c):
        tt, rows = at(c)
        return pltpu.make_async_remote_copy(
            src_ref=obuf.at[:, tt, levels - 1, rows, :],
            dst_ref=zin.at[:, tt, rows, :],
            send_sem=zs.at[c], recv_sem=zr.at[c],
            device_id={"lev": lax.rem(lev + 1, depth)}, device_id_type=pl.DeviceIdType.MESH,
        )

    def own_in(c):
        tt, rows = at(c)
        return pltpu.make_async_copy(
            x_ref.at[me * mine + tt, :, rows, :], recv.at[me, tt, :, rows, :], own1.at[c])

    def own_out(c):
        tt, rows = at(c)
        return pltpu.make_async_copy(
            obuf.at[me, tt, :, rows, :], out_ref.at[me * mine + tt, :, rows, :], own2.at[c])

    barrier = pltpu.get_barrier_semaphore()
    for k in range(1, n):
        pl.semaphore_signal(barrier, inc=1, device_id={"lon": peer(k)},
                            device_id_type=pl.DeviceIdType.MESH)
    for k in (1, depth - 1):
        pl.semaphore_signal(barrier, inc=1, device_id={"lev": lax.rem(lev + k, depth)},
                            device_id_type=pl.DeviceIdType.MESH)
    pl.semaphore_wait(barrier, n + 1)

    count = mine * halves

    @pl.loop(0, count)
    def _(c):
        own_in(c).start()

        @pl.loop(1, n)
        def _(k):
            outward(c, k).start()

    @pl.loop(0, lats)
    def _(j):
        shift = jnp.full((1, width), offsets_ref[j], jnp.int32)
        row_ref[pl.ds(j, 1), :] = shift
        share_ref[pl.ds(j, 1), :] = jnp.full((1, width), fraction_ref[j], jnp.float32)

    def ratios(tracer):
        bin_class = jnp.full((SUB, width), class_ref[tracer // GROUPS], jnp.int32)
        speed = 0.5
        for b in range(3):
            speed = speed * jnp.where((bin_class & (1 << b)) != 0, 2.0 ** (1 << b), 1.0)
        return [speed / thick_ref[level] for level in range(levels)]

    lane = lax.broadcasted_iota(jnp.int32, (SUB, width), 1)

    def behind(value, by):
        by %= n
        if by == 0:
            return value
        return jnp.concatenate([value[n - by:], value[:n - by]], axis=0)

    def turn(c):
        tt = c // halves
        base = (c % halves) * rows_of
        ratio = ratios(me * mine + tt)
        keep = [1.0 / (1.0 + r) for r in ratio]
        carry = [r * k for r, k in zip(ratio, keep)]
        own_in(c).wait()

        @pl.loop(1, n)
        def _(k):
            outward(c, k).wait_recv()

        @pl.loop(0, rows_of // SUB)
        def _(g):
            rows = pl.ds(pl.multiple_of(base + g * SUB, SUB), SUB)
            shift = row_ref[rows, :]
            remainder = lax.rem(shift, width)
            quotient = lax.div(shift, width)
            share = share_ref[rows, :]
            fine = [(remainder & (1 << b)) != 0 for b in range((width - 1).bit_length())]
            coarse = [(quotient & (1 << b)) != 0 for b in range((n - 1).bit_length())]
            same_block = lane >= remainder
            first_lane = lane == 0
            value = None
            for level in range(levels):
                field = recv[:, tt, level, rows, :]
                turned = pltpu.roll(field, 1, axis=2)
                left = jnp.where(first_lane[None], behind(turned, 1), turned)
                field = (1.0 - share)[None] * field + share[None] * left
                for b, chosen in enumerate(fine):
                    field = jnp.where(chosen[None], pltpu.roll(field, 1 << b, axis=2), field)
                field = jnp.where(same_block[None], field, behind(field, 1))
                for b, chosen in enumerate(coarse):
                    field = jnp.where(chosen[None], behind(field, 1 << b), field)
                field = keep[level][None] * field
                value = field if value is None else field + carry[level][None] * value
                obuf[:, tt, level, rows, :] = value

    def settle(c):
        tt = c // halves
        base = (c % halves) * rows_of
        reach = []
        for r in ratios(me * mine + tt):
            step = r / (1.0 + r)
            reach.append(reach[-1] * step if reach else step)

        def add_above(level):
            @pl.loop(0, rows_of // SUB)
            def _(g):
                rows = pl.ds(pl.multiple_of(base + g * SUB, SUB), SUB)
                obuf[:, tt, level, rows, :] += reach[level][None] * zin[:, tt, rows, :]

        @pl.when(lev > 0)
        def _():
            downward(c).wait_recv()
            add_above(levels - 1)

        @pl.when(lev < depth - 1)
        def _():
            downward(c).start()

        @pl.when(lev > 0)
        def _():
            for level in range(levels - 1):
                add_above(level)

    def send_home(c):
        own_out(c).start()

        @pl.loop(1, n)
        def _(k):
            homeward(c, k).start()

    hold = min(HOLD, count - 1)

    @pl.loop(0, count + depth - 1)
    def _(i):
        @pl.when(i < count)
        def _():
            turn(i)

        done = i - lev

        @pl.when((done >= 0) & (done < count))
        def _():
            settle(done)

        @pl.when((done >= 0) & (done < count) & (i > hold))
        def _():
            send_home(done)

        @pl.when(i == hold)
        def _():
            @pl.loop(0, count)
            def _(c):
                @pl.when(c <= done)
                def _():
                    send_home(c)

    @pl.loop(0, count)
    def _(c):
        own_out(c).wait()

        @pl.when(lev < depth - 1)
        def _():
            downward(c).wait_send()

        @pl.loop(1, n)
        def _(k):
            outward(c, k).wait_send()
            homeward(c, k).wait()


def on_device(tracers, offsets, fraction, bin_class, thickness):
    count, levels, lats, width = tracers.shape
    n = lax.axis_size("lon")
    depth = lax.axis_size("lev")
    mine = count // n
    pieces = mine * max(1, min(PIECES // mine, lats // SUB))
    smem = pl.BlockSpec(memory_space=pltpu.SMEM)
    sem = pltpu.SemaphoreType.DMA
    return pl.pallas_call(
        functools.partial(exchange_kernel, n, depth),
        out_shape=jax.ShapeDtypeStruct(tracers.shape, jnp.float32),
        in_specs=[pl.BlockSpec(memory_space=pltpu.HBM), smem, smem, smem, smem],
        out_specs=pl.BlockSpec(memory_space=pl.ANY),
        scratch_shapes=[
            pltpu.VMEM((n, mine, levels, lats, width), jnp.float32),
            pltpu.VMEM((n, mine, levels, lats, width), jnp.float32),
            pltpu.VMEM((n, mine, lats, width), jnp.float32),
            pltpu.VMEM((lats, width), jnp.int32),
            pltpu.VMEM((lats, width), jnp.float32),
            sem((pieces, n)), sem((pieces, n)), sem((pieces, n)), sem((pieces, n)),
            sem((pieces,)), sem((pieces,)), sem((pieces,)), sem((pieces,)),
        ],
        compiler_params=pltpu.CompilerParams(
            collective_id=0, has_side_effects=True, vmem_limit_bytes=58 << 20),
    )(tracers, offsets, fraction, bin_class, thickness)


def solution(mesh):
    in_specs = (P(None, "lev", None, "lon"), P(), P(), P(), P("lev"))
    out_specs = P(None, "lev", None, "lon")
    return jax.shard_map(
        on_device, mesh=mesh, in_specs=in_specs, out_specs=out_specs, check_vma=False
    )
```

```python
import functools

import jax
import jax.numpy as jnp
from jax import lax
from jax.experimental import pallas as pl
from jax.experimental.pallas import tpu as pltpu
from jax.sharding import PartitionSpec as P

GROUPS = 4
SUB = 8
PIECES = 8
HOLD = 5


def exchange_kernel(
    n, depth, x_ref, offsets_hbm, fraction_hbm, class_hbm, thick_hbm, out_ref,
    offsets_ref, fraction_ref, class_ref, thick_ref, small, recv, obuf, zin, row_ref, share_ref, s1, r1, s2, r2, own1, own2, zs, zr,
):
    tracers, levels, lats, width = x_ref.shape
    mine = tracers // n
    halves = max(1, min(PIECES // mine, lats // SUB))
    rows_of = lats // halves
    me = lax.axis_index("lon")
    lev = lax.axis_index("lev")

    def at(c):
        return c // halves, pl.ds(pl.multiple_of((c % halves) * rows_of, SUB), rows_of)

    def peer(k):
        return lax.rem(me + k, n)

    def outward(c, k):
        tt, rows = at(c)
        return pltpu.make_async_remote_copy(
            src_ref=x_ref.at[peer(k) * mine + tt, :, rows, :],
            dst_ref=recv.at[me, tt, :, rows, :],
            send_sem=s1.at[c, k], recv_sem=r1.at[c, k],
            device_id={"lon": peer(k)}, device_id_type=pl.DeviceIdType.MESH,
        )

    def homeward(c, k):
        tt, rows = at(c)
        return pltpu.make_async_remote_copy(
            src_ref=obuf.at[peer(k), tt, :, rows, :],
            dst_ref=out_ref.at[me * mine + tt, :, rows, :],
            send_sem=s2.at[c, k], recv_sem=r2.at[c, k],
            device_id={"lon": peer(k)}, device_id_type=pl.DeviceIdType.MESH,
        )

    def downward(c):
        tt, rows = at(c)
        return pltpu.make_async_remote_copy(
            src_ref=obuf.at[:, tt, levels - 1, rows, :],
            dst_ref=zin.at[:, tt, rows, :],
            send_sem=zs.at[c], recv_sem=zr.at[c],
            device_id={"lev": lax.rem(lev + 1, depth)}, device_id_type=pl.DeviceIdType.MESH,
        )

    def own_in(c):
        tt, rows = at(c)
        return pltpu.make_async_copy(
            x_ref.at[me * mine + tt, :, rows, :], recv.at[me, tt, :, rows, :], own1.at[c])

    def own_out(c):
        tt, rows = at(c)
        return pltpu.make_async_copy(
            obuf.at[me, tt, :, rows, :], out_ref.at[me * mine + tt, :, rows, :], own2.at[c])

    scalars = [
        pltpu.make_async_copy(source, held, small.at[i])
        for i, (source, held) in enumerate((
            (offsets_hbm, offsets_ref), (fraction_hbm, fraction_ref),
            (class_hbm, class_ref), (thick_hbm, thick_ref)))
    ]
    for copy in scalars:
        copy.start()

    barrier = pltpu.get_barrier_semaphore()
    for k in range(1, n):
        pl.semaphore_signal(barrier, inc=1, device_id={"lon": peer(k)},
                            device_id_type=pl.DeviceIdType.MESH)
    for k in (1, depth - 1):
        pl.semaphore_signal(barrier, inc=1, device_id={"lev": lax.rem(lev + k, depth)},
                            device_id_type=pl.DeviceIdType.MESH)
    pl.semaphore_wait(barrier, n + 1)

    count = mine * halves

    @pl.loop(0, count)
    def _(c):
        own_in(c).start()

        @pl.loop(1, n)
        def _(k):
            outward(c, k).start()

    for copy in scalars:
        copy.wait()

    @pl.loop(0, lats)
    def _(j):
        shift = jnp.full((1, width), offsets_ref[j], jnp.int32)
        row_ref[pl.ds(j, 1), :] = shift
        share_ref[pl.ds(j, 1), :] = jnp.full((1, width), fraction_ref[j], jnp.float32)

    def ratios(tracer):
        bin_class = jnp.full((SUB, width), class_ref[tracer // GROUPS], jnp.int32)
        speed = 0.5
        for b in range(3):
            speed = speed * jnp.where((bin_class & (1 << b)) != 0, 2.0 ** (1 << b), 1.0)
        return [speed / thick_ref[level] for level in range(levels)]

    lane = lax.broadcasted_iota(jnp.int32, (SUB, width), 1)

    def behind(value, by):
        by %= n
        if by == 0:
            return value
        return jnp.concatenate([value[n - by:], value[:n - by]], axis=0)

    def turn(c):
        tt = c // halves
        base = (c % halves) * rows_of
        ratio = ratios(me * mine + tt)
        keep = [1.0 / (1.0 + r) for r in ratio]
        carry = [r * k for r, k in zip(ratio, keep)]
        own_in(c).wait()

        @pl.loop(1, n)
        def _(k):
            outward(c, k).wait_recv()

        @pl.loop(0, rows_of // SUB)
        def _(g):
            rows = pl.ds(pl.multiple_of(base + g * SUB, SUB), SUB)
            shift = row_ref[rows, :]
            remainder = lax.rem(shift, width)
            quotient = lax.div(shift, width)
            share = share_ref[rows, :]
            fine = [(remainder & (1 << b)) != 0 for b in range((width - 1).bit_length())]
            coarse = [(quotient & (1 << b)) != 0 for b in range((n - 1).bit_length())]
            same_block = lane >= remainder
            first_lane = lane == 0
            value = None
            for level in range(levels):
                field = recv[:, tt, level, rows, :]
                turned = pltpu.roll(field, 1, axis=2)
                left = jnp.where(first_lane[None], behind(turned, 1), turned)
                field = (1.0 - share)[None] * field + share[None] * left
                for b, chosen in enumerate(fine):
                    field = jnp.where(chosen[None], pltpu.roll(field, 1 << b, axis=2), field)
                field = jnp.where(same_block[None], field, behind(field, 1))
                for b, chosen in enumerate(coarse):
                    field = jnp.where(chosen[None], behind(field, 1 << b), field)
                field = keep[level][None] * field
                value = field if value is None else field + carry[level][None] * value
                obuf[:, tt, level, rows, :] = value

    def settle(c):
        tt = c // halves
        base = (c % halves) * rows_of
        reach = []
        for r in ratios(me * mine + tt):
            step = r / (1.0 + r)
            reach.append(reach[-1] * step if reach else step)

        def add_above(level):
            @pl.loop(0, rows_of // SUB)
            def _(g):
                rows = pl.ds(pl.multiple_of(base + g * SUB, SUB), SUB)
                obuf[:, tt, level, rows, :] += reach[level][None] * zin[:, tt, rows, :]

        @pl.when(lev > 0)
        def _():
            downward(c).wait_recv()
            add_above(levels - 1)

        @pl.when(lev < depth - 1)
        def _():
            downward(c).start()

        @pl.when(lev > 0)
        def _():
            for level in range(levels - 1):
                add_above(level)

    def send_home(c):
        own_out(c).start()

        @pl.loop(1, n)
        def _(k):
            homeward(c, k).start()

    hold = min(HOLD, count - 1)

    @pl.loop(0, count + depth - 1)
    def _(i):
        @pl.when(i < count)
        def _():
            turn(i)

        done = i - lev

        @pl.when((done >= 0) & (done < count))
        def _():
            settle(done)

        @pl.when((done >= 0) & (done < count) & (i > hold))
        def _():
            send_home(done)

        @pl.when(i == hold)
        def _():
            @pl.loop(0, count)
            def _(c):
                @pl.when(c <= done)
                def _():
                    send_home(c)

    @pl.loop(0, count)
    def _(c):
        own_out(c).wait()

        @pl.when(lev < depth - 1)
        def _():
            downward(c).wait_send()

        @pl.loop(1, n)
        def _(k):
            outward(c, k).wait_send()
            homeward(c, k).wait()


def on_device(tracers, offsets, fraction, bin_class, thickness):
    count, levels, lats, width = tracers.shape
    n = lax.axis_size("lon")
    depth = lax.axis_size("lev")
    mine = count // n
    pieces = mine * max(1, min(PIECES // mine, lats // SUB))
    hbm = pl.BlockSpec(memory_space=pltpu.HBM)
    held = [pltpu.SMEM(a.shape, a.dtype) for a in (offsets, fraction, bin_class, thickness)]
    sem = pltpu.SemaphoreType.DMA
    return pl.pallas_call(
        functools.partial(exchange_kernel, n, depth),
        out_shape=jax.ShapeDtypeStruct(tracers.shape, jnp.float32),
        in_specs=[hbm] * 5,
        out_specs=pl.BlockSpec(memory_space=pl.ANY),
        scratch_shapes=[
            *held, sem((4,)),
            pltpu.VMEM((n, mine, levels, lats, width), jnp.float32),
            pltpu.VMEM((n, mine, levels, lats, width), jnp.float32),
            pltpu.VMEM((n, mine, lats, width), jnp.float32),
            pltpu.VMEM((lats, width), jnp.int32),
            pltpu.VMEM((lats, width), jnp.float32),
            sem((pieces, n)), sem((pieces, n)), sem((pieces, n)), sem((pieces, n)),
            sem((pieces,)), sem((pieces,)), sem((pieces,)), sem((pieces,)),
        ],
        compiler_params=pltpu.CompilerParams(
            collective_id=0, has_side_effects=True, vmem_limit_bytes=24 << 20),
    )(*(pltpu.with_memory_space_constraint(a, pltpu.HBM)
        for a in (tracers, offsets, fraction, bin_class, thickness)))


def solution(mesh):
    in_specs = (P(None, "lev", None, "lon"), P(), P(), P(), P("lev"))
    out_specs = P(None, "lev", None, "lon")
    return jax.shard_map(
        on_device, mesh=mesh, in_specs=in_specs, out_specs=out_specs, check_vma=False
    )
```

```python
import functools

import jax
import jax.numpy as jnp
from jax import lax
from jax.experimental import pallas as pl
from jax.experimental.pallas import tpu as pltpu
from jax.sharding import PartitionSpec as P

GROUPS = 4
SUB = 8
PIECES = 8
HOLD = 3


def exchange_kernel(
    n, depth, x_ref, offsets_hbm, fraction_hbm, class_hbm, thick_hbm, out_ref,
    offsets_ref, fraction_ref, class_ref, thick_ref, small, recv, obuf, zin, row_ref, share_ref, s1, r1, s2, r2, own1, own2, zs, zr,
):
    tracers, levels, lats, width = x_ref.shape
    mine = tracers // n
    halves = max(1, min(PIECES // mine, lats // SUB))
    rows_of = lats // halves
    me = lax.axis_index("lon")
    lev = lax.axis_index("lev")

    def at(c):
        return c // halves, pl.ds(pl.multiple_of((c % halves) * rows_of, SUB), rows_of)

    def peer(k):
        return lax.rem(me + k, n)

    def outward(tt, k):
        return pltpu.make_async_remote_copy(
            src_ref=x_ref.at[peer(k) * mine + tt],
            dst_ref=recv.at[me, tt],
            send_sem=s1.at[tt, k], recv_sem=r1.at[tt, k],
            device_id={"lon": peer(k)}, device_id_type=pl.DeviceIdType.MESH,
        )

    def homeward(tt, k):
        return pltpu.make_async_remote_copy(
            src_ref=obuf.at[peer(k), tt],
            dst_ref=out_ref.at[me * mine + tt],
            send_sem=s2.at[tt, k], recv_sem=r2.at[tt, k],
            device_id={"lon": peer(k)}, device_id_type=pl.DeviceIdType.MESH,
        )

    def downward(c):
        tt, rows = at(c)
        return pltpu.make_async_remote_copy(
            src_ref=obuf.at[:, tt, levels - 1, rows, :],
            dst_ref=zin.at[:, tt, rows, :],
            send_sem=zs.at[c], recv_sem=zr.at[c],
            device_id={"lev": lax.rem(lev + 1, depth)}, device_id_type=pl.DeviceIdType.MESH,
        )

    def own_in(tt):
        return pltpu.make_async_copy(x_ref.at[me * mine + tt], recv.at[me, tt], own1.at[tt])

    def own_out(tt):
        return pltpu.make_async_copy(obuf.at[me, tt], out_ref.at[me * mine + tt], own2.at[tt])

    scalars = [
        pltpu.make_async_copy(source, held, small.at[i])
        for i, (source, held) in enumerate((
            (offsets_hbm, offsets_ref), (fraction_hbm, fraction_ref),
            (class_hbm, class_ref), (thick_hbm, thick_ref)))
    ]
    for copy in scalars:
        copy.start()

    barrier = pltpu.get_barrier_semaphore()
    for k in range(1, n):
        pl.semaphore_signal(barrier, inc=1, device_id={"lon": peer(k)},
                            device_id_type=pl.DeviceIdType.MESH)
    for k in (1, depth - 1):
        pl.semaphore_signal(barrier, inc=1, device_id={"lev": lax.rem(lev + k, depth)},
                            device_id_type=pl.DeviceIdType.MESH)
    pl.semaphore_wait(barrier, n + 1)

    count = mine * halves

    @pl.loop(0, mine)
    def _(tt):
        @pl.loop(1, n)
        def _(k):
            outward(tt, k).start()

        own_in(tt).start()

    for copy in scalars:
        copy.wait()

    @pl.loop(0, lats)
    def _(j):
        shift = jnp.full((1, width), offsets_ref[j], jnp.int32)
        row_ref[pl.ds(j, 1), :] = shift
        share_ref[pl.ds(j, 1), :] = jnp.full((1, width), fraction_ref[j], jnp.float32)

    def ratios(tracer):
        bin_class = jnp.full((SUB, width), class_ref[tracer // GROUPS], jnp.int32)
        speed = 0.5
        for b in range(3):
            speed = speed * jnp.where((bin_class & (1 << b)) != 0, 2.0 ** (1 << b), 1.0)
        return [speed / thick_ref[level] for level in range(levels)]

    lane = lax.broadcasted_iota(jnp.int32, (SUB, width), 1)

    def behind(value, by):
        by %= n
        if by == 0:
            return value
        return jnp.concatenate([value[n - by:], value[:n - by]], axis=0)

    def turn(c):
        tt = c // halves
        base = (c % halves) * rows_of
        ratio = ratios(me * mine + tt)
        keep = [1.0 / (1.0 + r) for r in ratio]
        carry = [r * k for r, k in zip(ratio, keep)]

        @pl.when(c % halves == 0)
        def _():
            own_in(tt).wait()

            @pl.loop(1, n)
            def _(k):
                outward(tt, k).wait_recv()

        @pl.loop(0, rows_of // SUB)
        def _(g):
            rows = pl.ds(pl.multiple_of(base + g * SUB, SUB), SUB)
            shift = row_ref[rows, :]
            remainder = lax.rem(shift, width)
            quotient = lax.div(shift, width)
            share = share_ref[rows, :]
            fine = [(remainder & (1 << b)) != 0 for b in range((width - 1).bit_length())]
            coarse = [(quotient & (1 << b)) != 0 for b in range((n - 1).bit_length())]
            same_block = lane >= remainder
            first_lane = lane == 0
            value = None
            for level in range(levels):
                field = recv[:, tt, level, rows, :]
                turned = pltpu.roll(field, 1, axis=2)
                left = jnp.where(first_lane[None], behind(turned, 1), turned)
                field = (1.0 - share)[None] * field + share[None] * left
                for b, chosen in enumerate(fine):
                    field = jnp.where(chosen[None], pltpu.roll(field, 1 << b, axis=2), field)
                field = jnp.where(same_block[None], field, behind(field, 1))
                for b, chosen in enumerate(coarse):
                    field = jnp.where(chosen[None], behind(field, 1 << b), field)
                field = keep[level][None] * field
                value = field if value is None else field + carry[level][None] * value
                obuf[:, tt, level, rows, :] = value

    def settle(c):
        tt = c // halves
        base = (c % halves) * rows_of
        reach = []
        for r in ratios(me * mine + tt):
            step = r / (1.0 + r)
            reach.append(reach[-1] * step if reach else step)

        def add_above(level):
            @pl.loop(0, rows_of // SUB)
            def _(g):
                rows = pl.ds(pl.multiple_of(base + g * SUB, SUB), SUB)
                obuf[:, tt, level, rows, :] += reach[level][None] * zin[:, tt, rows, :]

        @pl.when(lev > 0)
        def _():
            downward(c).wait_recv()
            add_above(levels - 1)

        @pl.when(lev < depth - 1)
        def _():
            downward(c).start()

        @pl.when(lev > 0)
        def _():
            for level in range(levels - 1):
                add_above(level)

    def send_home(tt):
        @pl.loop(1, n)
        def _(k):
            homeward(tt, k).start()

        own_out(tt).start()

    hold = min(HOLD, count - 1)

    @pl.loop(0, count + depth - 1)
    def _(i):
        @pl.when(i < count)
        def _():
            turn(i)

        done = i - lev

        @pl.when((done >= 0) & (done < count))
        def _():
            settle(done)

        @pl.when((done >= 0) & (done < count) & (done % halves == halves - 1) & (i > hold))
        def _():
            send_home(done // halves)

        @pl.when(i == hold)
        def _():
            @pl.loop(0, mine)
            def _(tt):
                @pl.when((tt + 1) * halves - 1 <= done)
                def _():
                    send_home(tt)

    @pl.when(lev < depth - 1)
    def _():
        @pl.loop(0, count)
        def _(c):
            downward(c).wait_send()

    @pl.loop(0, mine)
    def _(tt):
        own_out(tt).wait()

        @pl.loop(1, n)
        def _(k):
            outward(tt, k).wait_send()
            homeward(tt, k).wait()


def on_device(tracers, offsets, fraction, bin_class, thickness):
    count, levels, lats, width = tracers.shape
    n = lax.axis_size("lon")
    depth = lax.axis_size("lev")
    mine = count // n
    pieces = mine * max(1, min(PIECES // mine, lats // SUB))
    hbm = pl.BlockSpec(memory_space=pltpu.HBM)
    held = [pltpu.SMEM(a.shape, a.dtype) for a in (offsets, fraction, bin_class, thickness)]
    sem = pltpu.SemaphoreType.DMA
    return pl.pallas_call(
        functools.partial(exchange_kernel, n, depth),
        out_shape=jax.ShapeDtypeStruct(tracers.shape, jnp.float32),
        in_specs=[hbm] * 5,
        out_specs=pl.BlockSpec(memory_space=pl.ANY),
        scratch_shapes=[
            *held, sem((4,)),
            pltpu.VMEM((n, mine, levels, lats, width), jnp.float32),
            pltpu.VMEM((n, mine, levels, lats, width), jnp.float32),
            pltpu.VMEM((n, mine, lats, width), jnp.float32),
            pltpu.VMEM((lats, width), jnp.int32),
            pltpu.VMEM((lats, width), jnp.float32),
            sem((mine, n)), sem((mine, n)), sem((mine, n)), sem((mine, n)),
            sem((mine,)), sem((mine,)), sem((pieces,)), sem((pieces,)),
        ],
        compiler_params=pltpu.CompilerParams(
            collective_id=0, has_side_effects=True, vmem_limit_bytes=24 << 20),
    )(*(pltpu.with_memory_space_constraint(a, pltpu.HBM)
        for a in (tracers, offsets, fraction, bin_class, thickness)))


def solution(mesh):
    in_specs = (P(None, "lev", None, "lon"), P(), P(), P(), P("lev"))
    out_specs = P(None, "lev", None, "lon")
    return jax.shard_map(
        on_device, mesh=mesh, in_specs=in_specs, out_specs=out_specs, check_vma=False
    )
```
